32 devices in a mesh: groups: 2 (over y), mp: 4 (over x, core), hidden: 4 (over z).
Axes of the slice: x: 2, y: 2, z: 4, core: 2. Of those that a mesh axis runs over, the one named last changes fastest.
Arguments:
- inputs: bfloat16 [2048, 8192], P(('groups', 'hidden'), 'mp'), parts along dimension 0, as said below
- out_grad: bfloat16 [2048, 16384], P(('groups', 'mp'), 'hidden'), parts along dimension 0, as said below
- weight: float32 [8192, 16384], P('mp', 'hidden'), may hold values from -0.0625 to 0.0625
- noise: bfloat16 [2, 16384, 16384], P(None, ('groups', 'mp'), 'hidden'), parts along dimension 1, may hold values from -6 to 6
Outputs:
- outputs: bfloat16 [2048, 16384], P(('groups', 'mp'), 'hidden'), parts along dimension 0
- in_grad: bfloat16 [2048, 8192], P(('groups', 'hidden'), 'mp'), parts along dimension 0
- update: float32 [8192, 32768], P('mp', ('groups', 'hidden')), parts along dimension 1
The draws below stay inside these ranges and needn't reach their ends.
There are 2 independent parts, one for each index of `groups`. The reference program is written for one: setup_inputs(seed, part) draws one part's arguments, and reference() takes and returns one part's arrays. A program takes and returns all parts, laid end to end along the dimension named above; an argument that names none is the same for every part. Nothing has to cross between parts.
Inputs may be any that keep to these rules, and one draw needn't show every extreme that they name: `inputs`: Real-valued activations whose rows and columns carry independent scales. `out_grad`: Real-valued gradients whose rows and columns carry independent scales; examples differ in overall size.
All inputs are finite; a program needn't handle non-finite values.
Results may differ from the reference program's by a relative error of at most 0.0049.
Values may be sent and summed in bfloat16 or wider, within the bound.
A program may use at most 256 MiB of HBM per device.

```python
import math
import jax
import jax.numpy as jnp
from jax import lax

D = 8192
FF = 16384
SEQ = 64
EXAMPLES = 16


def column_scales(key, columns):
    spot = jnp.arange(columns, dtype=jnp.float32) / max(columns - 1, 1)
    jitter = jax.random.uniform(key, (columns,), jnp.float32, 0.0, math.log(3.5))
    return jnp.exp(math.log(3.0) * spot + jitter) / 3.0


def base_field(key, shape):
    first_key = jax.random.fold_in(key, 0)
    return jax.random.normal(first_key, shape, jnp.float32)


def draw_inputs(key, part):
    first_key, second_key, third_key = jax.random.split(jax.random.fold_in(key, 11), 3)
    total = EXAMPLES * SEQ
    values = base_field(first_key, (total, D))
    row_scale = jnp.exp(jax.random.uniform(second_key, (total, 1), jnp.float32, math.log(0.3), math.log(3.0)))
    return (values * row_scale * column_scales(third_key, D)[None, :]).astype(jnp.bfloat16)


def draw_out_grad(key, part):
    first_key, second_key, third_key, fourth_key, fifth_key = jax.random.split(jax.random.fold_in(key, 23), 5)
    total = EXAMPLES * SEQ
    values = base_field(first_key, (total, FF))
    row_scale = jnp.exp(jax.random.uniform(second_key, (total, 1), jnp.float32, math.log(0.3), math.log(3.0)))
    ranking = jax.random.permutation(third_key, EXAMPLES).astype(jnp.float32)
    jitter = jax.random.uniform(fourth_key, (EXAMPLES,), jnp.float32, 0.0, 1.0)
    example_scale = jnp.power(10.0, -(ranking + jitter) / EXAMPLES)
    token_scale = jnp.repeat(example_scale, SEQ)[:, None]
    return (values * row_scale * token_scale * column_scales(fifth_key, FF)[None, :]).astype(jnp.bfloat16)


def block_levels(stream_key, dims, pieces, smallest, top_value):
    level, own = 1.0, jax.random.fold_in(stream_key, 6)
    for axis_at, shards_of in pieces:
        heights = jnp.exp(jax.random.uniform(jax.random.fold_in(own, axis_at), (shards_of,), jnp.float32, smallest / len(pieces), top_value / len(pieces)))
        level = level * jnp.repeat(heights, dims[axis_at] // shards_of).reshape([-1 if axis == axis_at else 1 for axis in range(len(dims))])
    return level


def bell_draw(stream_key, dims, width, most, shards=(), kind=jnp.bfloat16):
    array = jax.random.normal(stream_key, dims, jnp.float32) * width
    if len(shards) > 0:
        array = block_levels(stream_key, dims, shards, -0.22, 0.18) * array
    return jnp.clip(array, min=-most, max=most).astype(kind)


def setup_inputs(seed: int = 0, part: int = 0) -> dict:
    streams_of = jax.random.split(jax.random.key(seed), 5)
    part_keys = jax.random.split(jax.random.fold_in(streams_of[4], part), 5)
    inputs = draw_inputs(jax.random.fold_in(jax.random.fold_in(streams_of[4], part), 71), part)
    out_grad = draw_out_grad(jax.random.fold_in(jax.random.fold_in(streams_of[4], part), 71), part)
    weight = bell_draw(streams_of[2], (D, FF), D ** -0.5, 0.0625, ((0, 4), (1, 4)), jnp.float32)
    noise = bell_draw(part_keys[3], (2, D, FF), 1.0, 6.0, ((1, 4), (2, 4)))
    return {"inputs": inputs, "out_grad": out_grad, "weight": weight, "noise": noise}


def reference(inputs, out_grad, weight, noise):
    weight_half = weight.astype(jnp.bfloat16)
    outputs = jnp.dot(inputs, weight_half, preferred_element_type=jnp.float32).astype(jnp.bfloat16)
    in_grad = jnp.dot(out_grad, weight_half.T, preferred_element_type=jnp.float32).astype(jnp.bfloat16)
    feature_blocks = inputs.astype(jnp.float32).reshape(EXAMPLES, SEQ, D)
    unit_blocks = out_grad.astype(jnp.float32).reshape(EXAMPLES, SEQ, FF)
    feature_gram = jnp.einsum('bsd,btd->bst', feature_blocks, feature_blocks, precision=lax.Precision.HIGHEST)
    unit_gram = jnp.einsum('bsd,btd->bst', unit_blocks, unit_blocks, precision=lax.Precision.HIGHEST)
    squares = lax.optimization_barrier(jnp.sum(feature_gram * unit_gram, axis=(1, 2)))
    clip_norm = math.sqrt(SEQ * D * FF)
    factor = jnp.minimum(1.0, clip_norm / jnp.sqrt(squares + 1e-06))
    scaled_grad = (unit_blocks * factor[:, None, None]).reshape(EXAMPLES * SEQ, FF).astype(jnp.bfloat16)
    weight_grad = jnp.dot(inputs.T, scaled_grad, preferred_element_type=jnp.float32)
    band_noise = noise[0].astype(jnp.float32) - 0.6 * noise[1].astype(jnp.float32)
    update = (weight_grad * (math.sqrt(D * FF) / clip_norm) + 4.0 * band_noise) / EXAMPLES
    return (outputs, in_grad, update)
```

```python
import math

import jax
import jax.numpy as jnp
from jax import lax
from jax.experimental import pallas as pl
from jax.experimental.pallas import tpu as pltpu
from jax.sharding import PartitionSpec as P


D = 8192
FF = 16384
SEQ = 64
EXAMPLES = 16
PARTS = 4


def ring_up(value, axis, n):
    return lax.ppermute(value, axis, [(i, (i + 1) % n) for i in range(n)])


def swap(value, axis, n, bit):
    return lax.ppermute(value, axis, [(i, i ^ bit) for i in range(n)])


def bits(n):
    return [1 << i for i in range(n.bit_length() - 1)]


def after(value, event):
    return lax.optimization_barrier((value, event))[0]


def put(buffer, block, index):
    return lax.dynamic_update_slice(buffer, block, (index * block.shape[0], 0))


def take(buffer, index, rows):
    return lax.dynamic_slice_in_dim(buffer, index * rows, rows, axis=0)


def update_kernel(gain, features_ref, grad_ref, noise_ref, *rest):
    out_ref = rest[-1]
    weight_grad = jnp.dot(
        features_ref[...], grad_ref[...], preferred_element_type=jnp.float32
    )
    band = noise_ref[0].astype(jnp.float32) - 0.6 * noise_ref[1].astype(jnp.float32)
    out_ref[...] = (weight_grad * gain + 4.0 * band) * (1.0 / EXAMPLES)


def update_part(features_t, scaled_grad, noise, gain, part, parts, so_far):
    m, tokens = features_t.shape
    n = scaled_grad.shape[1]
    tm, tn = min(m, 512), min(n // parts, 1024)
    steps = n // parts // tn
    at = part * steps
    in_specs = [
        pl.BlockSpec((tm, tokens), lambda j, i: (i, 0)),
        pl.BlockSpec((tokens, tn), lambda j, i: (0, at + j)),
        pl.BlockSpec((2, tm, tn), lambda j, i: (0, i, at + j)),
    ]
    operands = [features_t, scaled_grad, noise]
    aliases = {}
    if so_far is not None:
        in_specs.append(pl.BlockSpec(memory_space=pl.ANY))
        operands.append(so_far)
        aliases = {3: 0}
    return pl.pallas_call(
        lambda *refs: update_kernel(gain, *refs),
        grid=(steps, m // tm),
        in_specs=in_specs,
        out_specs=pl.BlockSpec((tm, tn), lambda j, i: (i, at + j)),
        out_shape=jax.ShapeDtypeStruct((m, n), jnp.float32),
        input_output_aliases=aliases,
        cost_estimate=pl.CostEstimate(
            flops=2 * m * n * tokens // parts,
            bytes_accessed=12 * m * n // parts,
            transcendentals=0,
        ),
        compiler_params=pltpu.CompilerParams(vmem_limit_bytes=40 * 1024 * 1024),
    )(*operands)


def block_gram(rows):
    blocks = rows.reshape(-1, SEQ, rows.shape[1])
    return jnp.einsum("bsd,btd->bst", blocks, blocks, preferred_element_type=jnp.float32)


def shards(n_mp, n_hidden, inputs, out_grad, weight, noise):
    mp, hidden = lax.axis_index("mp"), lax.axis_index("hidden")
    in_rows, width = inputs.shape
    out_rows, units = out_grad.shape
    tokens = in_rows * n_hidden

    have = {0: out_grad}
    bit = n_mp // 2
    while bit:
        have.update({o ^ bit: swap(v, "mp", n_mp, bit) for o, v in have.items()})
        bit //= 2

    weight_half = lax.optimization_barrier(weight.astype(jnp.bfloat16))

    feature_rows = jnp.zeros((tokens, width), jnp.bfloat16)
    partial = jnp.zeros((tokens, units), jnp.bfloat16)
    block = inputs
    events = []
    for step in range(n_hidden):
        at = lax.rem(hidden - step + n_hidden, n_hidden)
        later = None
        if step < n_hidden - 1:
            later = ring_up(block, "hidden", n_hidden)
        product = jnp.dot(block, weight_half, preferred_element_type=jnp.float32)
        partial = put(partial, product.astype(jnp.bfloat16), at)
        feature_rows = put(feature_rows, block, at)
        block = later
        if later is not None:
            events.append(later)

    def event(index):
        return events[min(index, len(events) - 1)][:8, :128]

    unit_rows = jnp.zeros((tokens, units), jnp.bfloat16)
    for offset, value in have.items():
        unit_rows = put(unit_rows, value, mp ^ offset)

    own = in_rows % SEQ == 0 and in_rows == out_rows
    if own:
        feature_gram, unit_gram = block_gram(inputs), block_gram(out_grad)
        for k, bit in enumerate(bits(n_mp)):
            arrived = after(swap(feature_gram, "mp", n_mp, bit), event(k))
            feature_gram = feature_gram + arrived
        for k, bit in enumerate(bits(n_hidden)):
            arrived = after(swap(unit_gram, "hidden", n_hidden, bit), event(k))
            unit_gram = unit_gram + arrived
        mine = jnp.sum(feature_gram * unit_gram, axis=(1, 2))
        mine = jnp.where(mp == hidden, mine, 0.0)
        squares = lax.dynamic_update_slice(
            jnp.zeros((tokens // SEQ,), jnp.float32), mine, (hidden * (in_rows // SEQ),)
        )
        for bit in bits(n_mp):
            squares = squares + after(swap(squares, "mp", n_mp, bit), event(2))

    first = partial.reshape(-1, 2, out_rows, units)
    mine = lax.rem(mp, 2)
    keep = lax.dynamic_index_in_dim(first, mine, 1, keepdims=False)
    send = lax.dynamic_index_in_dim(first, 1 - mine, 1, keepdims=False)
    near = swap(send, "mp", n_mp, 1)

    pieces = 2
    columns = width // pieces
    shares = []
    operand = unit_rows
    for piece in range(pieces):
        share = lax.dot_general(
            operand,
            weight_half[piece * columns : (piece + 1) * columns],
            (((1,), (1,)), ((), ())),
            preferred_element_type=jnp.float32,
        )
        shares.append(lax.optimization_barrier(share))
        if piece == 0:
            near = after(near, shares[0][:8, :128])
            left = (keep.astype(jnp.float32) + near.astype(jnp.float32)).astype(jnp.bfloat16)
            operand = after(unit_rows, left[0, :8, :128])
    bit = 2
    while bit < n_mp:
        pairs = left.reshape(-1, 2, out_rows, units)
        mine = lax.rem(mp // bit, 2)
        keep = lax.dynamic_index_in_dim(pairs, mine, 1, keepdims=False)
        send = lax.dynamic_index_in_dim(pairs, 1 - mine, 1, keepdims=False)
        arrived = swap(send, "mp", n_mp, bit)
        left = (keep.astype(jnp.float32) + arrived.astype(jnp.float32)).astype(jnp.bfloat16)
        bit *= 2
    outputs = left.reshape(out_rows, units)

    done = []
    for piece in range(pieces):
        running = None
        for step in range(n_hidden):
            at = lax.rem(hidden - 1 - step + 2 * n_hidden, n_hidden)
            term = take(shares[piece], at, in_rows)
            if step:
                arrived = ring_up(running, "hidden", n_hidden)
                term = term + arrived.astype(jnp.float32)
            running = term.astype(jnp.bfloat16)
        done.append(running)
    in_grad = jnp.concatenate(done, axis=1)

    if own:
        for bit in bits(n_hidden):
            arrived = after(swap(squares, "hidden", n_hidden, bit), shares[0][:8, :128])
            squares = squares + arrived
    if not own:
        feature_gram = lax.psum(block_gram(feature_rows).astype(jnp.bfloat16), "mp").astype(jnp.float32)
        unit_gram = lax.psum(block_gram(unit_rows).astype(jnp.bfloat16), "hidden").astype(jnp.float32)
        squares = jnp.sum(feature_gram * unit_gram, axis=(1, 2))
    clip_norm = math.sqrt(SEQ * D * FF)
    factor = jnp.minimum(1.0, clip_norm / jnp.sqrt(squares + 1e-06))
    token_factor = jnp.repeat(factor, SEQ)[:, None]
    scaled_grad = (unit_rows.astype(jnp.float32) * token_factor).astype(jnp.bfloat16)
    features_t = feature_rows.T
    gain = math.sqrt(D * FF) / clip_norm
    parts = PARTS if units % (PARTS * 1024) == 0 else 1
    update = None
    for part in range(parts):
        update = update_part(features_t, scaled_grad, noise, gain, part, parts, update)
    return (outputs, in_grad, update)


def solution(mesh):
    n_mp, n_hidden = mesh.shape["mp"], mesh.shape["hidden"]
    in_specs = (
        P(("groups", "hidden"), "mp"),
        P(("groups", "mp"), "hidden"),
        P("mp", "hidden"),
        P(None, ("groups", "mp"), "hidden"),
    )
    out_specs = (
        P(("groups", "mp"), "hidden"),
        P(("groups", "hidden"), "mp"),
        P("mp", ("groups", "hidden")),
    )

    def body(*args):
        return shards(n_mp, n_hidden, *args)

    return jax.shard_map(body, mesh=mesh, in_specs=in_specs, out_specs=out_specs, check_vma=False)
```

```python
import math

import jax
import jax.numpy as jnp
from jax import lax
from jax.experimental import pallas as pl
from jax.experimental.pallas import tpu as pltpu
from jax.sharding import PartitionSpec as P


D = 8192
FF = 16384
SEQ = 64
EXAMPLES = 16
PARTS = 4


def ring_up(value, axis, n):
    return lax.ppermute(value, axis, [(i, (i + 1) % n) for i in range(n)])


def swap(value, axis, n, bit):
    return lax.ppermute(value, axis, [(i, i ^ bit) for i in range(n)])


def bits(n):
    return [1 << i for i in range(n.bit_length() - 1)]


def after(value, event):
    return lax.optimization_barrier((value, event))[0]


def put(buffer, block, index):
    return lax.dynamic_update_slice(buffer, block, (index * block.shape[0], 0))


def take(buffer, index, rows):
    return lax.dynamic_slice_in_dim(buffer, index * rows, rows, axis=0)


def update_kernel(gain, features_ref, grad_ref, noise_ref, *rest):
    out_ref = rest[-1]
    weight_grad = jnp.dot(
        features_ref[...], grad_ref[...], preferred_element_type=jnp.float32
    )
    band = noise_ref[0].astype(jnp.float32) - 0.6 * noise_ref[1].astype(jnp.float32)
    out_ref[...] = (weight_grad * gain + 4.0 * band) * (1.0 / EXAMPLES)


def update_part(features_t, scaled_grad, noise, gain, part, parts, so_far):
    m, tokens = features_t.shape
    n = scaled_grad.shape[1]
    tm, tn = min(m, 512), min(n // parts, 1024)
    steps = n // parts // tn
    at = part * steps
    in_specs = [
        pl.BlockSpec((tm, tokens), lambda j, i: (i, 0)),
        pl.BlockSpec((tokens, tn), lambda j, i: (0, at + j)),
        pl.BlockSpec((2, tm, tn), lambda j, i: (0, i, at + j)),
    ]
    operands = [features_t, scaled_grad, noise]
    aliases = {}
    if so_far is not None:
        in_specs.append(pl.BlockSpec(memory_space=pl.ANY))
        operands.append(so_far)
        aliases = {3: 0}
    return pl.pallas_call(
        lambda *refs: update_kernel(gain, *refs),
        grid=(steps, m // tm),
        in_specs=in_specs,
        out_specs=pl.BlockSpec((tm, tn), lambda j, i: (i, at + j)),
        out_shape=jax.ShapeDtypeStruct((m, n), jnp.float32),
        input_output_aliases=aliases,
        cost_estimate=pl.CostEstimate(
            flops=2 * m * n * tokens // parts,
            bytes_accessed=12 * m * n // parts,
            transcendentals=0,
        ),
        compiler_params=pltpu.CompilerParams(vmem_limit_bytes=40 * 1024 * 1024),
    )(*operands)


def block_gram(rows):
    blocks = rows.reshape(-1, SEQ, rows.shape[1])
    return jnp.einsum("bsd,btd->bst", blocks, blocks, preferred_element_type=jnp.float32)


def shards(n_mp, n_hidden, inputs, out_grad, weight, noise):
    mp, hidden = lax.axis_index("mp"), lax.axis_index("hidden")
    in_rows, width = inputs.shape
    out_rows, units = out_grad.shape
    tokens = in_rows * n_hidden

    have = {0: out_grad}
    bit = n_mp // 2
    while bit:
        have.update({o ^ bit: swap(v, "mp", n_mp, bit) for o, v in have.items()})
        bit //= 2

    weight_half = lax.optimization_barrier(weight.astype(jnp.bfloat16))

    feature_rows = jnp.zeros((tokens, width), jnp.bfloat16)
    partial = jnp.zeros((tokens, units), jnp.bfloat16)
    block = inputs
    events = []
    for step in range(n_hidden):
        at = lax.rem(hidden - step + n_hidden, n_hidden)
        later = None
        if step < n_hidden - 1:
            later = ring_up(block, "hidden", n_hidden)
        product = jnp.dot(block, weight_half, preferred_element_type=jnp.float32)
        partial = put(partial, product.astype(jnp.bfloat16), at)
        feature_rows = put(feature_rows, block, at)
        block = later
        if later is not None:
            events.append(later)

    def event(index):
        return events[min(index, len(events) - 1)][:8, :128]

    unit_rows = jnp.zeros((tokens, units), jnp.bfloat16)
    for offset, value in have.items():
        unit_rows = put(unit_rows, value, mp ^ offset)

    own = in_rows % SEQ == 0 and in_rows == out_rows
    if own:
        feature_gram, unit_gram = block_gram(inputs), block_gram(out_grad)
        for k, bit in enumerate(bits(n_mp)):
            arrived = after(swap(feature_gram, "mp", n_mp, bit), event(k))
            feature_gram = feature_gram + arrived
        for k, bit in enumerate(bits(n_hidden)):
            arrived = after(swap(unit_gram, "hidden", n_hidden, bit), event(k))
            unit_gram = unit_gram + arrived
        mine = jnp.sum(feature_gram * unit_gram, axis=(1, 2))
        mine = jnp.where(mp == hidden, mine, 0.0)
        squares = lax.dynamic_update_slice(
            jnp.zeros((tokens // SEQ,), jnp.float32), mine, (hidden * (in_rows // SEQ),)
        )
        for bit in bits(n_mp):
            squares = squares + after(swap(squares, "mp", n_mp, bit), event(2))

    first = partial.reshape(-1, 2, out_rows, units)
    mine = lax.rem(mp, 2)
    keep = lax.dynamic_index_in_dim(first, mine, 1, keepdims=False)
    send = lax.dynamic_index_in_dim(first, 1 - mine, 1, keepdims=False)
    near = swap(send, "mp", n_mp, 1)

    pieces = 2
    columns = width // pieces
    shares = []
    for piece in range(pieces):
        share = lax.dot_general(
            unit_rows,
            weight_half[piece * columns : (piece + 1) * columns],
            (((1,), (1,)), ((), ())),
            preferred_element_type=jnp.float32,
        )
        shares.append(lax.optimization_barrier(share))
    left = (keep.astype(jnp.float32) + near.astype(jnp.float32)).astype(jnp.bfloat16)
    bit = 2
    while bit < n_mp:
        pairs = left.reshape(-1, 2, out_rows, units)
        mine = lax.rem(mp // bit, 2)
        keep = lax.dynamic_index_in_dim(pairs, mine, 1, keepdims=False)
        send = lax.dynamic_index_in_dim(pairs, 1 - mine, 1, keepdims=False)
        arrived = swap(send, "mp", n_mp, bit)
        left = (keep.astype(jnp.float32) + arrived.astype(jnp.float32)).astype(jnp.bfloat16)
        bit *= 2
    outputs = left.reshape(out_rows, units)

    done = []
    for piece in range(pieces):
        running = None
        for step in range(n_hidden):
            at = lax.rem(hidden - 1 - step + 2 * n_hidden, n_hidden)
            term = take(shares[piece], at, in_rows)
            if step:
                arrived = ring_up(running, "hidden", n_hidden)
                term = term + arrived.astype(jnp.float32)
            running = term.astype(jnp.bfloat16)
        done.append(running)
    in_grad = jnp.concatenate(done, axis=1)

    if own:
        for bit in bits(n_hidden):
            arrived = after(swap(squares, "hidden", n_hidden, bit), shares[0][:8, :128])
            squares = squares + arrived
    if not own:
        feature_gram = lax.psum(block_gram(feature_rows).astype(jnp.bfloat16), "mp").astype(jnp.float32)
        unit_gram = lax.psum(block_gram(unit_rows).astype(jnp.bfloat16), "hidden").astype(jnp.float32)
        squares = jnp.sum(feature_gram * unit_gram, axis=(1, 2))
    clip_norm = math.sqrt(SEQ * D * FF)
    factor = jnp.minimum(1.0, clip_norm / jnp.sqrt(squares + 1e-06))
    token_factor = jnp.repeat(factor, SEQ)[:, None]
    scaled_grad = (unit_rows.astype(jnp.float32) * token_factor).astype(jnp.bfloat16)
    features_t = feature_rows.T
    gain = math.sqrt(D * FF) / clip_norm
    parts = PARTS if units % (PARTS * 1024) == 0 else 1
    update = None
    for part in range(parts):
        update = update_part(features_t, scaled_grad, noise, gain, part, parts, update)
    return (outputs, in_grad, update)


def solution(mesh):
    n_mp, n_hidden = mesh.shape["mp"], mesh.shape["hidden"]
    in_specs = (
        P(("groups", "hidden"), "mp"),
        P(("groups", "mp"), "hidden"),
        P("mp", "hidden"),
        P(None, ("groups", "mp"), "hidden"),
    )
    out_specs = (
        P(("groups", "mp"), "hidden"),
        P(("groups", "hidden"), "mp"),
        P("mp", ("groups", "hidden")),
    )

    def body(*args):
        return shards(n_mp, n_hidden, *args)

    return jax.shard_map(body, mesh=mesh, in_specs=in_specs, out_specs=out_specs, check_vma=False)
```
